32 devices in a mesh: dp: 8 (over z, x), tensor: 4 (over y, core).
Axes of the slice: x: 2, y: 2, z: 4, core: 2. Of those that a mesh axis runs over, the one named last changes fastest.
Arguments:
- attn_out: bfloat16 [4096, 8192], P('dp', 'tensor'), may hold values from -6 to 6
- frozen_weight: bfloat16 [8192, 8192], P('tensor', 'dp'), may hold values from -0.0625 to 0.0625
- vector_bank: float32 [256, 256], replicated, may hold values from -0.18 to 0.18
- logits_a: float32 [16, 32, 2], P(None, 'tensor'), may hold values from -2 to 2
- index_a: int32 [16, 32, 2], P(None, 'tensor'), may hold values from 0 to 255, all different within a row
- logits_b: float32 [16, 32, 2], P(None, 'tensor'), may hold values from -2 to 2
- index_b: int32 [16, 32, 2], P(None, 'tensor'), may hold values from 0 to 255, all different within a row
- out_grad: bfloat16 [4096, 8192], P('dp'), may hold values from -6 to 6
Outputs:
- layer_out: bfloat16 [4096, 8192], P('dp', 'tensor')
- attn_grad: bfloat16 [4096, 8192], P('dp', 'tensor')
- bank_grad: float32 [256, 256], replicated
- logits_a_grad: float32 [16, 32, 2], P(None, 'tensor')
- logits_b_grad: float32 [16, 32, 2], P(None, 'tensor')
The draws below stay inside these ranges and needn't reach their ends.
Inputs may be any that keep to these rules, and one draw needn't show every extreme that they name: `index_a`: the 2 entries of one sub-vector differ. `index_b`: the 2 entries of one sub-vector differ.
All inputs are finite; a program needn't handle non-finite values.
Results may differ from the reference program's by a relative error of at most 0.014.
Values may be sent and summed in bfloat16 or wider, within the bound.
A program may use at most 128 MiB of HBM per device.

```python
import jax
import jax.numpy as jnp
from jax import lax

D = 8192
ATTN = 8192
RANK = 16
SUBLEN = 256
BANK = 256
TOP = 2
TOKENS = 4096
JA = 32
JB = 32
N_TENSOR = 4


def block_levels(own_key, extent, cuts, low, top_value):
    gain = 1.0
    for position, blocks in cuts:
        draws = jax.random.uniform(jax.random.fold_in(jax.random.fold_in(own_key, 6), position), (blocks,), jnp.float32, low / len(cuts), top_value / len(cuts))
        gain = gain * jnp.repeat(jnp.exp(draws), extent[position] // blocks).reshape((-1,) + (1,) * (len(extent) - 1 - position))
    return gain


def choose_distinct(stream_key, rows, number_of, top, lift):
    sequence = jax.random.permutation(jax.random.fold_in(stream_key, 1), number_of)
    boost = sequence
    for power in range(3):
        boost = boost * boost // number_of
    boost = boost * lift // number_of
    lots = jax.random.randint(jax.random.fold_in(stream_key, 2), (rows, number_of), 0, 4096) + boost
    fixed_rows = jax.random.permutation(jax.random.fold_in(stream_key, 3), rows)[jnp.arange(number_of) % rows]
    lots = jnp.where(jnp.arange(rows)[:, None] == fixed_rows[None, :], 1 << 14, lots)
    priority = lots * number_of + jnp.arange(number_of)
    return lax.top_k(priority.astype(jnp.int32), top)[1].astype(jnp.int32)


def normal_values(stream_key, shape, spread, bound, pieces=(), held_as=jnp.bfloat16):
    entries = jax.random.normal(stream_key, shape, jnp.float32) * spread
    if len(pieces) > 0:
        entries = block_levels(stream_key, shape, pieces, -0.22, 0.18) * entries
    return jnp.clip(entries, min=-bound, max=bound).astype(held_as)


def setup_inputs(seed: int = 0) -> dict:
    keys = jax.random.split(jax.random.key(seed), 9)
    attn_out = normal_values(keys[0], (TOKENS, ATTN), 1.0, 6.0, ((0, 8), (1, 4)))
    frozen_weight = normal_values(keys[1], (ATTN, D), ATTN ** -0.5, 0.0625, ((0, 4), (1, 8)))
    vector_bank = normal_values(keys[2], (BANK, SUBLEN), 0.03, 0.18, (), jnp.float32)
    logits_a = jnp.clip(jax.random.uniform(keys[3], (RANK, JA, TOP), jnp.float32, -2.0, 2.0) * block_levels(keys[3], (RANK, JA, TOP), ((1, 4),), -0.4, 0.0), -2.0, 2.0)
    index_a = choose_distinct(keys[4], RANK * JA, BANK, TOP, 64).reshape((RANK, JA, TOP))
    logits_b = jnp.clip(jax.random.uniform(keys[5], (RANK, JB, TOP), jnp.float32, -2.0, 2.0) * block_levels(keys[5], (RANK, JB, TOP), ((1, 4),), -0.4, 0.0), -2.0, 2.0)
    index_b = choose_distinct(keys[6], RANK * JB, BANK, TOP, 64).reshape((RANK, JB, TOP))
    out_grad = normal_values(keys[7], (TOKENS, D), 1.0, 6.0, ((0, 8),))
    return {"attn_out": attn_out, "frozen_weight": frozen_weight, "vector_bank": vector_bank, "logits_a": logits_a, "index_a": index_a, "logits_b": logits_b, "index_b": index_b, "out_grad": out_grad}


adapter_scale = 2.0


def compose(logits, indices, vector_bank):
    weights = jax.nn.sigmoid(logits - logits[..., ::-1])
    levels = jnp.arange(vector_bank.shape[0], dtype=jnp.int32)
    picked = (indices[..., None] == levels).astype(jnp.float32)
    mixing = jnp.sum(picked * weights[..., None], axis=2)
    blocks = jnp.einsum("rjb,bc->rjc", mixing, vector_bank, precision=lax.Precision.HIGHEST)
    return weights, picked, mixing, blocks.reshape(blocks.shape[0], -1)


def compose_back(grad_rows, weights, picked, mixing, vector_bank):
    blocks = grad_rows.reshape(mixing.shape[0], mixing.shape[1], -1)
    bank_part = jnp.einsum("rjb,rjc->bc", mixing, blocks, precision=lax.Precision.HIGHEST)
    projected = jnp.einsum("rjc,bc->rjb", blocks, vector_bank, precision=lax.Precision.HIGHEST)
    dots = jnp.sum(picked * projected[:, :, None, :], axis=3)
    logit_grad = weights * (dots - jnp.sum(weights * dots, axis=2, keepdims=True))
    return bank_part, logit_grad


def reference(attn_out, frozen_weight, vector_bank, logits_a, index_a, logits_b, index_b, out_grad):
    weights_a, picked_a, mixing_a, rows_a = compose(logits_a, index_a, vector_bank)
    weights_b, picked_b, mixing_b, rows_b = compose(logits_b, index_b, vector_bank)
    down_a = rows_a.astype(jnp.bfloat16)
    up_b = rows_b.astype(jnp.bfloat16)
    low_bf = jnp.dot(attn_out, down_a.T, preferred_element_type=jnp.float32).astype(jnp.bfloat16)
    back_bf = jnp.dot(out_grad, up_b.T, preferred_element_type=jnp.float32).astype(jnp.bfloat16)
    width = ATTN // N_TENSOR

    def add_block(carry, block):
        columns = lax.dynamic_slice_in_dim(attn_out, block * width, width, 1)
        weight_rows = lax.dynamic_slice_in_dim(frozen_weight, block * width, width, 0)
        partial_value = jnp.dot(columns, weight_rows, preferred_element_type=jnp.float32).astype(jnp.bfloat16)
        partial_value = lax.optimization_barrier(partial_value)
        return carry + partial_value.astype(jnp.float32), None

    summed, _ = lax.scan(add_block, jnp.zeros((attn_out.shape[0], D), jnp.float32), jnp.arange(N_TENSOR, dtype=jnp.int32))
    layer_out = (summed + adapter_scale * jnp.dot(low_bf, up_b, preferred_element_type=jnp.float32)).astype(jnp.bfloat16)
    main = lax.dot_general(out_grad, frozen_weight, (((1,), (1,)), ((), ())), preferred_element_type=jnp.float32)
    attn_grad = (main + adapter_scale * jnp.dot(back_bf, down_a, preferred_element_type=jnp.float32)).astype(jnp.bfloat16)
    factor = adapter_scale / TOKENS
    grad_a = factor * lax.dot_general(back_bf, attn_out, (((0,), (0,)), ((), ())), preferred_element_type=jnp.float32)
    grad_b = factor * lax.dot_general(low_bf, out_grad, (((0,), (0,)), ((), ())), preferred_element_type=jnp.float32)
    bank_a, logit_grad_a = compose_back(grad_a, weights_a, picked_a, mixing_a, vector_bank)
    bank_b, logit_grad_b = compose_back(grad_b, weights_b, picked_b, mixing_b, vector_bank)
    return layer_out, attn_grad, bank_a + bank_b, logit_grad_a, logit_grad_b
```

```python
import functools

import jax
import jax.numpy as jnp
from jax import lax
from jax.sharding import PartitionSpec as P

adapter_scale = 2.0
ROW_PIECES = 4


def compose(logits, indices, vector_bank):
    weights = jax.nn.sigmoid(logits - logits[..., ::-1])
    levels = jnp.arange(vector_bank.shape[0], dtype=jnp.int32)
    picked = (indices[..., None] == levels).astype(jnp.float32)
    mixing = jnp.sum(picked * weights[..., None], axis=2)
    blocks = jnp.einsum("rjb,bc->rjc", mixing, vector_bank, precision=lax.Precision.HIGHEST)
    return (weights, picked, mixing, blocks.reshape(blocks.shape[0], -1))


def compose_back(grad_rows, weights, picked, mixing, vector_bank):
    blocks = grad_rows.reshape(mixing.shape[0], mixing.shape[1], -1)
    bank_part = jnp.einsum("rjb,rjc->bc", mixing, blocks, precision=lax.Precision.HIGHEST)
    projected = jnp.einsum("rjc,bc->rjb", blocks, vector_bank, precision=lax.Precision.HIGHEST)
    dots = jnp.sum(picked * projected[:, :, None, :], axis=3)
    logit_grad = weights * (dots - jnp.sum(weights * dots, axis=2, keepdims=True))
    return (bank_part, logit_grad)


def local(attn_out, frozen_weight, vector_bank, logits_a, index_a, logits_b, index_b, out_grad):
    weights_a, picked_a, mixing_a, rows_a = compose(logits_a, index_a, vector_bank)
    weights_b, picked_b, mixing_b, rows_b = compose(logits_b, index_b, vector_bank)
    down_a = rows_a.astype(jnp.bfloat16)
    up_b = rows_b.astype(jnp.bfloat16)
    own_width = up_b.shape[1]
    grad_cols = lax.dynamic_slice_in_dim(
        out_grad, lax.axis_index("tensor") * own_width, own_width, 1
    )
    low_part = jnp.dot(attn_out, down_a.T, preferred_element_type=jnp.float32)
    back_part = jnp.dot(grad_cols, up_b.T, preferred_element_type=jnp.float32)
    low_total = lax.psum(low_part, "tensor")
    low_bf = low_total.astype(jnp.bfloat16)
    gathered = lax.all_gather(frozen_weight, "dp", axis=1, tiled=True)
    partial_value = jnp.dot(attn_out, gathered, preferred_element_type=jnp.float32).astype(
        jnp.bfloat16
    )
    summed = lax.psum_scatter(partial_value, "tensor", scatter_dimension=1, tiled=True).astype(
        jnp.float32
    )
    layer_out = (
        summed + adapter_scale * jnp.dot(low_bf, up_b, preferred_element_type=jnp.float32)
    ).astype(jnp.bfloat16)
    back_total = lax.psum(back_part, "tensor")
    back_bf = back_total.astype(jnp.bfloat16)
    main = lax.dot_general(
        out_grad, gathered, (((1,), (1,)), ((), ())), preferred_element_type=jnp.float32
    )
    attn_grad = (
        main + adapter_scale * jnp.dot(back_bf, down_a, preferred_element_type=jnp.float32)
    ).astype(jnp.bfloat16)
    factor = adapter_scale / (attn_out.shape[0] * lax.axis_size("dp"))
    grad_a = factor * lax.dot_general(
        back_bf, attn_out, (((0,), (0,)), ((), ())), preferred_element_type=jnp.float32
    )
    grad_b = factor * lax.dot_general(
        low_bf, grad_cols, (((0,), (0,)), ((), ())), preferred_element_type=jnp.float32
    )
    bank_a, logit_grad_a = compose_back(grad_a, weights_a, picked_a, mixing_a, vector_bank)
    bank_b, logit_grad_b = compose_back(grad_b, weights_b, picked_b, mixing_b, vector_bank)
    bank_part = bank_a + bank_b
    bank_group = lax.psum(bank_part, "tensor")
    bank_grad, logits_a_grad, logits_b_grad = lax.psum(
        (bank_group, logit_grad_a, logit_grad_b), "dp"
    )
    return (layer_out, attn_grad, bank_grad, logits_a_grad, logits_b_grad)


def ring_local(dp_size, tensor_size, attn_out, frozen_weight, vector_bank, logits_a, index_a, logits_b, index_b, out_grad):
    depth = tensor_size
    chips = tensor_size // 2
    rows = attn_out.shape[0]
    own_width = attn_out.shape[1]
    width = frozen_weight.shape[1]
    half = width // 2
    part = own_width // ROW_PIECES
    place = lax.axis_index("dp")
    level, side = place // 2, place % 2
    tensor_index = lax.axis_index("tensor")

    ring = [(d, (d + 2) % dp_size) for d in range(dp_size)]
    swap = [(d, d ^ 1) for d in range(dp_size)]

    def hop(value):
        return lax.ppermute(value, "dp", ring)

    def cross(value):
        return lax.ppermute(value, "dp", swap)

    def collect(partial_value, step):
        target = (level - step + depth) % depth
        pairs = []
        for d in range(dp_size):
            goal = (d // 2 - step) % depth
            for chip in range(chips):
                core = 2 * chip + goal % 2
                pairs.append((d * tensor_size + (core ^ 1), d * tensor_size + core))
        other = lax.ppermute(partial_value, ("dp", "tensor"), pairs)
        paired = partial_value.astype(jnp.float32) + other.astype(jnp.float32)
        sent = paired.astype(jnp.bfloat16)
        total = paired
        for k in range(1, chips):
            pairs = []
            for d in range(dp_size):
                goal = (d // 2 - step) % depth
                source = ((goal // 2 + k) % chips) * 2 + goal % 2
                pairs.append((d * tensor_size + source, d * tensor_size + goal))
            total = total + lax.ppermute(sent, ("dp", "tensor"), pairs).astype(jnp.float32)
        return jnp.where(tensor_index == target, total, 0.0)

    first = frozen_weight[:, :half]
    later = [frozen_weight[r * part : (r + 1) * part, half:] for r in range(ROW_PIECES)]
    held = [(first, later)]
    for step in range(1, depth):
        first = hop(first)
        later = [hop(v) for v in later]
        held.append((first, later))

    attn_two = jnp.concatenate([attn_out, cross(attn_out)], axis=0)
    attn_parts = [attn_two[:, r * part : (r + 1) * part] for r in range(ROW_PIECES)]

    def grad_pair(step):
        origin = (level - step + depth) % depth
        mine = lax.dynamic_slice_in_dim(out_grad, (origin * 2 + side) * width, width, 1)
        theirs = lax.dynamic_slice_in_dim(out_grad, (origin * 2 + 1 - side) * width, width, 1)
        return jnp.concatenate([mine, cross(theirs)], axis=0)

    weights_a, picked_a, mixing_a, rows_a = compose(logits_a, index_a, vector_bank)
    weights_b, picked_b, mixing_b, rows_b = compose(logits_b, index_b, vector_bank)
    down_a = rows_a.astype(jnp.bfloat16)
    up_b = rows_b.astype(jnp.bfloat16)
    rank = down_a.shape[0]
    grad_cols = lax.dynamic_slice_in_dim(out_grad, tensor_index * own_width, own_width, 1)
    low_part = jnp.dot(attn_out, down_a.T, preferred_element_type=jnp.float32)
    back_part = jnp.dot(grad_cols, up_b.T, preferred_element_type=jnp.float32)
    both = lax.psum(jnp.concatenate([low_part, back_part], axis=1), "tensor")
    low_bf = both[:, :rank].astype(jnp.bfloat16)
    back_bf = both[:, rank:].astype(jnp.bfloat16)

    sums = [None] * ROW_PIECES
    own_total = jnp.zeros((rows, width), jnp.float32)
    cross_total = jnp.zeros((rows, width), jnp.float32)
    for step in range(depth):
        first, later = held[step]
        grads = grad_pair(step)
        out_first = jnp.dot(attn_two, first, preferred_element_type=jnp.float32)
        for r in range(ROW_PIECES):
            term = lax.dot_general(
                grads[:, :half],
                first[r * part : (r + 1) * part],
                (((1,), (1,)), ((), ())),
                preferred_element_type=jnp.float32,
            )
            sums[r] = term if sums[r] is None else sums[r] + term
        out_later = None
        for r in range(ROW_PIECES):
            term = jnp.dot(attn_parts[r], later[r], preferred_element_type=jnp.float32)
            out_later = term if out_later is None else out_later + term
            sums[r] = sums[r] + lax.dot_general(
                grads[:, half:],
                later[r],
                (((1,), (1,)), ((), ())),
                preferred_element_type=jnp.float32,
            )
        out_first = out_first.astype(jnp.bfloat16)
        out_later = out_later.astype(jnp.bfloat16)
        if step < depth - 1:
            block = collect(jnp.concatenate([out_first, out_later], axis=1), step)
            own_total = own_total + block[:rows]
            cross_total = cross_total + block[rows:]
        if step == depth - 2:
            came = cross(cross_total.astype(jnp.bfloat16)).astype(jnp.float32)
        if step == depth - 1:
            ends = [collect(out_first, step), collect(out_later, step)]
            own_end = jnp.concatenate([v[:rows] for v in ends], axis=1)
            came_end = jnp.concatenate(
                [cross(v[rows:].astype(jnp.bfloat16)) for v in ends], axis=1
            ).astype(jnp.float32)
    own_half = own_total + own_end
    other_half = came + came_end
    summed = jnp.concatenate(
        [
            jnp.where(side == 0, own_half, other_half),
            jnp.where(side == 0, other_half, own_half),
        ],
        axis=1,
    )
    layer_out = (
        summed + adapter_scale * jnp.dot(low_bf, up_b, preferred_element_type=jnp.float32)
    ).astype(jnp.bfloat16)

    adapter = adapter_scale * jnp.dot(back_bf, down_a, preferred_element_type=jnp.float32)
    pieces = []
    for r in range(ROW_PIECES):
        came_grad = cross(sums[r][rows:].astype(jnp.bfloat16)).astype(jnp.float32)
        pieces.append(sums[r][:rows] + came_grad + adapter[:, r * part : (r + 1) * part])
    attn_grad = jnp.concatenate(pieces, axis=1).astype(jnp.bfloat16)

    factor = adapter_scale / (rows * dp_size)
    grad_a = factor * lax.dot_general(
        back_bf, attn_out, (((0,), (0,)), ((), ())), preferred_element_type=jnp.float32
    )
    grad_b = factor * lax.dot_general(
        low_bf, grad_cols, (((0,), (0,)), ((), ())), preferred_element_type=jnp.float32
    )
    bank_a, logit_grad_a = compose_back(grad_a, weights_a, picked_a, mixing_a, vector_bank)
    bank_b, logit_grad_b = compose_back(grad_b, weights_b, picked_b, mixing_b, vector_bank)
    bank_grad = lax.psum(bank_a + bank_b, ("dp", "tensor"))
    logits_a_grad, logits_b_grad = lax.psum((logit_grad_a, logit_grad_b), "dp")
    return (layer_out, attn_grad, bank_grad, logits_a_grad, logits_b_grad)


def solution(mesh):
    dp_size, tensor_size = mesh.shape["dp"], mesh.shape["tensor"]
    paired = dp_size == 2 * tensor_size and tensor_size % 2 == 0
    body = functools.partial(ring_local, dp_size, tensor_size) if paired else local
    return jax.shard_map(
        body,
        mesh=mesh,
        in_specs=(
            P("dp", "tensor"),
            P("tensor", "dp"),
            P(),
            P(None, "tensor", None),
            P(None, "tensor", None),
            P(None, "tensor", None),
            P(None, "tensor", None),
            P("dp", None),
        ),
        out_specs=(
            P("dp", "tensor"),
            P("dp", "tensor"),
            P(),
            P(None, "tensor", None),
            P(None, "tensor", None),
        ),
        check_vma=False,
    )
```
